256 devices in a mesh: row: 16 (over x, z_lo, core), col: 16 (over z_hi, y).
Axes of the slice: x: 4, y: 4, z: 8 (z_hi: 4, z_lo: 2; z = z_hi * 2 + z_lo), core: 2. Of those that a mesh axis runs over, the one named last changes fastest.
Arguments:
- amplitudes: bfloat16 [4, 1024, 1024], P(None, 'row', 'col'), may hold values from -6 to 6
- factors: bfloat16 [3072, 65536], P('col', 'row'), may hold values from -0.029907227 to 0.029907227
- tile_mask: int32 [16, 16], replicated, may hold values 0 or 1
- tile_irrep: int32 [16], replicated, may hold values from 0 to 1
Outputs:
- residual: float32 [4, 64, 64], P(None, 'row', 'col')
The draws below stay inside these ranges and needn't reach their ends.
All inputs are finite; a program needn't handle non-finite values.
Results may differ from the reference program's by a relative error of at most 0.007.
Values may be sent and summed in bfloat16 or wider, within the bound.
A program may use at most 128 MiB of HBM per device.

```python
import jax
import jax.numpy as jnp
from jax import lax

NV = 1024
NT = 16
TILE = 64
NQ = 3072
NOCC = 2
NPAIR = 4
WIN = 64


def place_ends(drawn, stream_key, low, largest):
    index_at = [jax.random.randint(jax.random.fold_in(stream_key, axis), (), 0, length) for axis, length in enumerate(drawn.shape)]
    main_axis = drawn.shape.index(max(drawn.shape))
    beside = index_at[:main_axis] + [(index_at[main_axis] + 1) % drawn.shape[main_axis]] + index_at[main_axis + 1:]
    return drawn.at[tuple(index_at)].set(low).at[tuple(beside)].set(largest)


def spiked(entries, own_key, source, target, shards_of, factor):
    def block_of(dim):
        return (jnp.arange(entries.shape[dim]) // (entries.shape[dim] // shards_of)).reshape((-1,) + (1,) * (entries.ndim - 1 - dim))

    first = jax.random.permutation(own_key, shards_of)[block_of(target)]
    far = (block_of(target) + shards_of // 2) % shards_of
    return jnp.where((block_of(source) == first) | (block_of(source) == far), factor * entries, entries)


def steps_of(key, shape, shards, least, largest):
    def one(axis_at, parts):
        draws = jax.random.uniform(jax.random.fold_in(jax.random.fold_in(key, 6), axis_at), (parts,), jnp.float32, least / len(shards), largest / len(shards))
        return jnp.repeat(jnp.exp(draws), shape[axis_at] // parts).reshape((-1,) + (1,) * (len(shape) - axis_at - 1))

    gain = one(*shards[0])
    for cut in shards[1:]:
        gain = gain * one(*cut)
    return gain


def bell_draw(key, shape, spread, reach, cuts=(), kind=jnp.bfloat16):
    drawn = spread * jax.random.normal(key, shape, jnp.float32)
    if cuts:
        drawn = drawn * steps_of(key, shape, cuts, -0.22, 0.18)
    return jnp.clip(drawn, -reach, reach).astype(kind)


def bell_draw_with(rng, dims, spread, most, split, heavy, kind=jnp.bfloat16):
    entries = spread * jax.random.normal(rng, dims, jnp.float32)
    if split:
        entries = entries * steps_of(rng, dims, split, -0.22, 0.18)
    return jnp.clip(spiked(entries, jax.random.fold_in(rng, 3), *heavy), -most, most).astype(kind)


def setup_inputs(seed: int = 0) -> dict:
    arg_keys = jax.random.split(jax.random.key(seed), 5)
    amplitudes = bell_draw(arg_keys[0], (NPAIR, NV, NV), 1.0, 6.0, ((1, 16), (2, 16)))
    factors = bell_draw_with(arg_keys[1], (NQ, NV * WIN), 0.005, 0.029907227, ((0, 16), (1, 16)), (0, 1, 16, 2.0))
    tile_mask = place_ends((jax.random.randint(arg_keys[2], (NT, NT), 0, 8) < 7).astype(jnp.int32), jax.random.fold_in(arg_keys[2], 1), 0, 1)
    tile_irrep = place_ends(jax.random.randint(arg_keys[3], (NT,), 0, 2), jax.random.fold_in(arg_keys[3], 1), 0, 1).astype(jnp.int32)
    return {"amplitudes": amplitudes, "factors": factors, "tile_mask": tile_mask, "tile_irrep": tile_irrep}


def reference(amplitudes, factors, tile_mask, tile_irrep):
    pair_index = jnp.arange(NPAIR, dtype=jnp.int32)
    first_occ = pair_index // NOCC
    second_occ = pair_index % NOCC
    pair_irrep = jnp.bitwise_xor(first_occ % 2, second_occ % 2).astype(jnp.int32)
    cross_irrep = jnp.bitwise_xor(tile_irrep[:, None], tile_irrep[None, :])
    live_tiles = tile_mask[None, :, :] * (cross_irrep[None, :, :] == pair_irrep[:, None, None]).astype(jnp.int32)
    shaped = amplitudes.reshape(NPAIR, NT, TILE, NT, TILE)
    masked = (shaped * live_tiles.astype(jnp.bfloat16)[:, :, None, :, None]).reshape(NPAIR, NT, TILE, NV)
    masked_wide = masked.astype(jnp.float32)
    q_block = 8

    def add_block(running, fac_block):
        near_side = fac_block.reshape(q_block, NT, TILE, WIN).astype(jnp.float32)
        partial_value = jnp.einsum('qkca,pkcd->qpkad', near_side, masked_wide)
        rounded = lax.optimization_barrier(partial_value.astype(jnp.bfloat16)).astype(jnp.float32)
        running = running + jnp.einsum('qpkad,qdb->pab', rounded, fac_block.astype(jnp.float32))
        return running, None

    start_sum = jnp.zeros((NPAIR, WIN, WIN), jnp.float32)
    ladder, _ = lax.scan(add_block, start_sum, factors.reshape(NQ // q_block, q_block, NV, WIN))
    mirror_term = ladder.reshape(NOCC, NOCC, WIN, WIN).transpose(1, 0, 3, 2).reshape(NPAIR, WIN, WIN)
    return ladder + mirror_term
```

```python
import functools

import jax
import jax.numpy as jnp
from jax import lax
from jax.experimental import pallas as pl
from jax.experimental.pallas import tpu as pltpu
from jax.sharding import PartitionSpec as P

TILE = 64
WIN = 64
MESH = pl.DeviceIdType.MESH
F32 = jnp.float32
BF16 = jnp.bfloat16


def greet(peers):
    barrier = pltpu.get_barrier_semaphore()
    for peer in peers:
        pl.semaphore_signal(barrier, inc=1, device_id=peer, device_id_type=MESH)
    pl.semaphore_wait(barrier, len(peers))


def row_swap(size, wide):
    at = lax.broadcasted_iota(jnp.int32, (size * size, size * size), 0)
    come = lax.broadcasted_iota(jnp.int32, (size * size, size * size), 1)
    hit = (at // size == come % size) & (at % size == come // size)
    return jnp.where(hit, 1.0, 0.0).astype(wide)


def regroup(fin, sbuf, g, swap):
    lane = lax.broadcasted_iota(jnp.int32, (16, 128), 1)
    low = lane < 64
    for jb in range(2):
        stacks = ([], [])
        for jj in range(16):
            cols = pl.ds(128 * (16 * jb + jj), 128)
            halves = ([], [])
            for kp in range(2):
                v0 = fin[pl.ds(64 * g + 32 * kp, 16), cols].astype(F32)
                v1 = fin[pl.ds(64 * g + 32 * kp + 16, 16), cols].astype(F32)
                halves[0].append(jnp.where(low, v0, pltpu.roll(v1, 64, 1)).astype(BF16))
                halves[1].append(jnp.where(low, pltpu.roll(v0, 64, 1), v1).astype(BF16))
            for e in range(2):
                stacks[e].append(jnp.concatenate(halves[e], axis=1))
        for e in range(2):
            moved = jnp.dot(swap, jnp.concatenate(stacks[e], axis=0), preferred_element_type=F32).astype(BF16)
            for r in range(16):
                sbuf[g, r, pl.ds(32 * e + 16 * jb, 16), :] = moved[16 * r : 16 * r + 16, :]


def share_kernel(f_hbm, fm, fin, sbuf, in_sem, send_sem, recv_sem, own_sem):
    row = lax.axis_index("row")
    col = lax.axis_index("col")
    loads = []
    for g in range(3):
        load = pltpu.make_async_copy(f_hbm.at[pl.ds(64 * g, 64)], fin.at[pl.ds(64 * g, 64)], in_sem.at[g])
        load.start()
        loads.append(load)
    greet([((row + o) % 16, col) for o in range(1, 16)])
    swap = row_swap(16, BF16)
    copies = []
    for g in range(3):
        loads[g].wait()
        regroup(fin, sbuf, g, swap)
        for o in range(1, 16):
            dest = (row + o) % 16
            copy = pltpu.make_async_remote_copy(
                src_ref=sbuf.at[g, dest],
                dst_ref=fm.at[g, row],
                send_sem=send_sem.at[g, o],
                recv_sem=recv_sem.at[g, o],
                device_id=(dest, col),
                device_id_type=MESH,
            )
            copy.start()
            copies.append(copy)
        own = pltpu.make_async_copy(sbuf.at[g, row], fm.at[g, row], own_sem.at[g])
        own.start()
        copies.append(own)
    for copy in copies:
        copy.wait()


def share(factors):
    return pl.pallas_call(
        share_kernel,
        out_shape=jax.ShapeDtypeStruct((3, 16, 64, 256), BF16),
        in_specs=[pl.BlockSpec(memory_space=pl.ANY)],
        out_specs=pl.BlockSpec(memory_space=pltpu.VMEM),
        scratch_shapes=[
            pltpu.VMEM((192, 4096), BF16),
            pltpu.VMEM((3, 16, 64, 256), BF16),
            pltpu.SemaphoreType.DMA((3,)),
            pltpu.SemaphoreType.DMA((3, 16)),
            pltpu.SemaphoreType.DMA((3, 16)),
            pltpu.SemaphoreType.DMA((3,)),
        ],
        compiler_params=pltpu.CompilerParams(collective_id=0, has_side_effects=True, vmem_limit_bytes=40 << 20),
        name="share_factors",
    )(factors)


def ladder_kernel(irrep, nt, lane_irrep, diag, fm, out, u0, u3, u1, xt, acc):
    lane = lax.broadcasted_iota(jnp.int32, (1, 1024), 1)
    lane2 = lax.broadcasted_iota(jnp.int32, (64, 128), 1)
    row2 = lax.broadcasted_iota(jnp.int32, (64, 128), 0)
    for t in range(16):
        rows = pl.ds(64 * t, 64)
        differs = jnp.abs(lane_irrep[...] - irrep[t].astype(F32))
        same = 1.0 - differs
        tile = nt[rows, :]
        u1[rows, :] = tile * differs.astype(BF16)
        u0[rows, :] = tile * jnp.where(lane < 64 * t, same, 0.0).astype(BF16)
        u3[rows, :] = tile * jnp.where(lane >= 64 * (t + 1), same, 0.0).astype(BF16)
        pair = pl.ds(128 * (t // 2), 128)
        here = nt[rows, pair]
        same_here = jnp.broadcast_to(1.0 - jnp.abs(lane_irrep[:, pair] - irrep[t].astype(F32)), (64, 128))
        offset = lane2 - 64 * (t % 2)
        in_tile = (offset >= 0) & (offset < 64)
        keep0 = (offset < 0) | (in_tile & (offset <= row2))
        keep3 = (offset >= 64) | (in_tile & (offset > row2))
        u0[rows, pair] = here * jnp.where(keep0, same_here, 0.0).astype(BF16)
        extra = jnp.where(offset == row2, jnp.broadcast_to(diag[:, pair], (64, 128)), 0.0)
        u3[rows, pair] = here * jnp.where(keep3, same_here, 0.0).astype(BF16) + extra.astype(BF16)
    acc[...] = jnp.zeros_like(acc)

    @pl.loop(0, 3)
    def _(g):
        near = fm.at[g]
        for i in range(4):
            rows = pl.ds(256 * i, 256)
            done = 256 * (i + 1)
            x0 = jnp.dot(u0[rows, :done], near[:done, :], preferred_element_type=F32)
            xt[rows, 0:256] = x0.astype(BF16)
            x3 = jnp.dot(u3[rows, 256 * i :], near[256 * i :, :], preferred_element_type=F32)
            xt[rows, 256:512] = x3.astype(BF16)
            x1 = jnp.dot(u1[rows, :], near[...], preferred_element_type=F32)
            xt[rows, 512:768] = x1.astype(BF16)
        acc[...] += lax.dot_general(near[...], xt[...], (((0,), (0,)), ((), ())), preferred_element_type=F32)

    for p in range(3):
        total = jnp.zeros((64, 64), F32)
        for k in range(4):
            total = total + acc[64 * k : 64 * k + 64, 256 * p + 64 * k : 256 * p + 64 * k + 64]
        out[p] = total


def ladder(irrep, nt, lane_irrep, diag, fm):
    vmem = pl.BlockSpec(memory_space=pltpu.VMEM)
    return pl.pallas_call(
        ladder_kernel,
        out_shape=jax.ShapeDtypeStruct((3, 64, 64), F32),
        in_specs=[pl.BlockSpec(memory_space=pltpu.SMEM), vmem, vmem, vmem, vmem],
        out_specs=vmem,
        scratch_shapes=[
            pltpu.VMEM((1024, 1024), BF16),
            pltpu.VMEM((1024, 1024), BF16),
            pltpu.VMEM((1024, 1024), BF16),
            pltpu.VMEM((1024, 768), BF16),
            pltpu.VMEM((256, 768), F32),
        ],
        compiler_params=pltpu.CompilerParams(vmem_limit_bytes=40 << 20),
        name="ladder_sums",
    )(irrep, nt, lane_irrep, diag, fm)


def reduce_kernel(g, out, send_a, recv_a, send_b, recv_b, sa, ra, sb, rb):
    row = lax.axis_index("row")
    col = lax.axis_index("col")
    greet([((row + o) % 16, col) for o in range(1, 16)] + [(row, (col + o) % 16) for o in range(1, 16)])
    near = (g[0] + g[0].T, g[2].T, g[2], g[1] + g[1].T)
    for r in range(16):
        for p in range(4):
            send_a[r, 4 * p : 4 * p + 4, :] = near[p][4 * r : 4 * r + 4, :]
    copies = []
    for o in range(1, 16):
        dest = (row + o) % 16
        copy = pltpu.make_async_remote_copy(
            src_ref=send_a.at[dest], dst_ref=recv_a.at[o], send_sem=sa.at[o], recv_sem=ra.at[o],
            device_id=(dest, col), device_id_type=MESH,
        )
        copy.start()
        copies.append(copy)
    total = send_a[row]
    for o in range(1, 16):
        copies[o - 1].wait_recv()
        total = total + recv_a[o]
    turned = total.T
    for c in range(16):
        send_b[c] = turned[4 * c : 4 * c + 4, :]
    for o in range(1, 16):
        dest = (col + o) % 16
        copy = pltpu.make_async_remote_copy(
            src_ref=send_b.at[dest], dst_ref=recv_b.at[o], send_sem=sb.at[o], recv_sem=rb.at[o],
            device_id=(row, dest), device_id_type=MESH,
        )
        copy.start()
        copies.append(copy)
    final = send_b[col]
    for o in range(1, 16):
        copies[14 + o].wait_recv()
        final = final + recv_b[o]
    back = final.T
    for p in range(4):
        out[p] = back[4 * p : 4 * p + 4, :]
    for copy in copies:
        copy.wait_send()


def reduce(partial):
    vmem = pl.BlockSpec(memory_space=pltpu.VMEM)
    sems = pltpu.SemaphoreType.DMA((16,))
    return pl.pallas_call(
        reduce_kernel,
        out_shape=jax.ShapeDtypeStruct((4, 4, 4), F32),
        in_specs=[vmem],
        out_specs=vmem,
        scratch_shapes=[
            pltpu.VMEM((16, 16, 64), F32),
            pltpu.VMEM((16, 16, 64), F32),
            pltpu.VMEM((16, 4, 16), F32),
            pltpu.VMEM((16, 4, 16), F32),
            sems, sems, sems, sems,
        ],
        compiler_params=pltpu.CompilerParams(collective_id=1, has_side_effects=True),
        name="reduce_ladder",
    )(partial)


def regrouped(matrix):
    return matrix.reshape(32, 2, 32, 2).transpose(1, 0, 3, 2).reshape(64, 64)


def per_device(amplitudes, factors, tile_mask, tile_irrep):
    row = lax.axis_index("row")
    col = lax.axis_index("col")
    crossed = jnp.bitwise_xor(tile_irrep[row], tile_irrep[col])
    stored = tile_mask[row, col].astype(F32)
    amps = amplitudes.astype(F32) * stored
    alike = crossed == 0
    kept = jnp.where(alike, jnp.where(row <= col, amps[0], amps[3]), amps[1])
    given = jnp.where(alike, jnp.where(row <= col, amps[3], amps[0]), amps[2])
    pairs = [(r * 16 + c, c * 16 + r) for r in range(16) for c in range(16)]
    got = lax.ppermute(given.astype(BF16), ("row", "col"), pairs).astype(F32)
    at = lax.broadcasted_iota(jnp.int32, (64, 64), 0)
    to = lax.broadcasted_iota(jnp.int32, (64, 64), 1)
    a0 = regrouped(amps[0])
    a3 = regrouped(amps[3])
    diagonal = jnp.where(at < to, a0 + a0.T, jnp.where(at > to, a3 + a3.T, a0))
    piece = jnp.where(row == col, diagonal, regrouped(kept) + regrouped(got).T)
    column = lax.all_gather(piece.T.astype(BF16), "row", axis=1, tiled=True)
    nt = lax.all_gather(column, "col", axis=0, tiled=True)
    own_diag = jnp.where(row == col, jnp.diagonal(a3), 0.0)
    diag = lax.psum(own_diag, "row")
    diag = lax.all_gather(diag, "col", axis=0, tiled=True).reshape(1, 1024)
    lane_irrep = jnp.repeat(tile_irrep.astype(F32), 64).reshape(1, 1024)
    fm = share(factors)
    partial = ladder(tile_irrep, nt, lane_irrep, diag, fm.reshape(3, 1024, 256))
    return reduce(partial)


def solution(mesh):
    return jax.shard_map(
        per_device,
        mesh=mesh,
        in_specs=(P(None, "row", "col"), P("col", "row"), P(), P()),
        out_specs=P(None, "row", "col"),
        check_vma=False,
    )
```

```python
import jax
import jax.numpy as jnp
from jax import lax
from jax.experimental import pallas as pl
from jax.experimental.pallas import tpu as pltpu
from jax.sharding import PartitionSpec as P

MESH = pl.DeviceIdType.MESH
F32 = jnp.float32
BF16 = jnp.bfloat16
NN = (((1,), (0,)), ((), ()))
NT_DIMS = (((1,), (1,)), ((), ()))
TN = (((0,), (0,)), ((), ()))


def product(left, right, dims=NN):
    return lax.dot_general(left, right, dims, preferred_element_type=F32)


def row_swap():
    at = lax.broadcasted_iota(jnp.int32, (256, 256), 0)
    come = lax.broadcasted_iota(jnp.int32, (256, 256), 1)
    hit = (at // 16 == come % 16) & (at % 16 == come // 16)
    return jnp.where(hit, 1.0, 0.0).astype(BF16)


def regroup(fin, sbuf, g, swap):
    low = lax.broadcasted_iota(jnp.int32, (16, 128), 1) < 64
    for jb in range(2):
        stacks = ([], [])
        for jj in range(16):
            cols = pl.ds(128 * (16 * jb + jj), 128)
            halves = ([], [])
            for kp in range(2):
                v0 = fin[pl.ds(64 * g + 32 * kp, 16), cols].astype(F32)
                v1 = fin[pl.ds(64 * g + 32 * kp + 16, 16), cols].astype(F32)
                halves[0].append(jnp.where(low, v0, pltpu.roll(v1, 64, 1)).astype(BF16))
                halves[1].append(jnp.where(low, pltpu.roll(v0, 64, 1), v1).astype(BF16))
            for e in range(2):
                stacks[e].append(jnp.concatenate(halves[e], axis=1))
        for e in range(2):
            moved = product(swap, jnp.concatenate(stacks[e], axis=0)).astype(BF16)
            for r in range(16):
                sbuf[g, r, pl.ds(32 * e + 16 * jb, 16), :] = moved[16 * r : 16 * r + 16, :]


def own_tiles(mask, irrep, amps, ktile, gtile, dvec, row, col):
    at = lax.broadcasted_iota(jnp.int32, (64, 64), 0)
    to = lax.broadcasted_iota(jnp.int32, (64, 64), 1)
    left = jnp.where(to == 2 * (at % 32) + at // 32, 1.0, 0.0).astype(BF16)
    at = lax.broadcasted_iota(jnp.int32, (64, 128), 0)
    to = lax.broadcasted_iota(jnp.int32, (64, 128), 1)
    within = to % 64
    right = jnp.where(at == 2 * (within % 32) + within // 32, 1.0, 0.0).astype(BF16)
    crossed = jnp.abs(irrep[row].astype(F32) - irrep[col].astype(F32))
    stored = mask[row, col].astype(F32)
    alike = stored * (1.0 - crossed)
    unlike = stored * crossed
    upper = (row <= col).astype(F32)
    lower = 1.0 - upper
    a0, a1, a2, a3 = (amps[p].astype(F32) for p in range(4))
    kept = ((alike * upper) * a0 + (alike * lower) * a3 + unlike * a1).astype(BF16)
    given = ((alike * upper) * a3 + (alike * lower) * a0 + unlike * a2).astype(BF16)
    kept_turned = product(product(left, kept, NT_DIMS).astype(BF16), right)
    kept_plain = product(product(left, kept).astype(BF16), right)
    given_turned = product(product(left, given, NT_DIMS).astype(BF16), right)
    given_plain = product(product(left, given).astype(BF16), right)
    both = jnp.where(
        within < at, kept_turned + kept_plain, jnp.where(within > at, given_turned + given_plain, kept_plain)
    )
    on_diagonal = (row == col).astype(F32)
    mine = on_diagonal * both + (1.0 - on_diagonal) * kept_turned
    half = to // 64
    mine = jnp.where(half == row % 2, mine, 0.0).astype(BF16)
    theirs = jnp.where(half == col % 2, given_plain, 0.0).astype(BF16)
    for h in range(2):
        ktile[h] = mine[32 * h : 32 * h + 32, :]
        gtile[h] = theirs[32 * h : 32 * h + 32, :]
    line = jnp.sum(jnp.where(within == at, given_plain, 0.0), axis=0, keepdims=True)
    dvec[...] = jnp.broadcast_to(line, (8, 128)).astype(BF16)


def split_matrix(irrep, nt, dall, u0, u3, u1):
    lane = lax.broadcasted_iota(jnp.int32, (1, 1024), 1)
    lane2 = lax.broadcasted_iota(jnp.int32, (64, 128), 1)
    row2 = lax.broadcasted_iota(jnp.int32, (64, 128), 0)
    lane_irrep = jnp.zeros((1, 1024), F32)
    for t in range(16):
        lane_irrep = jnp.where(lane // 64 == t, irrep[t].astype(F32), lane_irrep)
    for t in range(16):
        differs = jnp.abs(lane_irrep - irrep[t].astype(F32))
        same = 1.0 - differs
        pair = slice(128 * (t // 2), 128 * (t // 2) + 128)
        same_here = jnp.broadcast_to(same[:, pair], (64, 128))
        offset = lane2 - 64 * (t % 2)
        in_tile = (offset >= 0) & (offset < 64)
        keep0 = (offset < 0) | (in_tile & (offset <= row2))
        keep3 = (offset >= 64) | (in_tile & (offset > row2))
        extra = jnp.where(offset == row2, jnp.broadcast_to(dall[t, 0:1, :].astype(F32), (64, 128)), 0.0).astype(BF16)
        part0 = jnp.where(lane < 64 * t, same, 0.0).astype(BF16)
        part3 = jnp.where(lane >= 64 * (t + 1), same, 0.0).astype(BF16)
        part1 = differs.astype(BF16)
        here0 = jnp.where(keep0, same_here, 0.0).astype(BF16)
        here3 = jnp.where(keep3, same_here, 0.0).astype(BF16)
        for h in range(2):
            rows = pl.ds(64 * t + 32 * h, 32)
            sub = slice(32 * h, 32 * h + 32)
            tile = nt[2 * t + h]
            u1[rows, :] = tile * part1
            u0[rows, :] = tile * part0
            u3[rows, :] = tile * part3
            u0[rows, pair] = tile[:, pair] * here0[sub]
            u3[rows, pair] = tile[:, pair] * here3[sub] + extra[sub]


def chunk_sums(near, u0, u3, u1, xt, acc):
    for i in range(4):
        rows = pl.ds(256 * i, 256)
        done = 256 * (i + 1)
        xt[rows, 0:256] = product(u0[rows, :done], near[:done, :]).astype(BF16)
        xt[rows, 256:512] = product(u3[rows, 256 * i :], near[256 * i :, :]).astype(BF16)
        xt[rows, 512:768] = product(u1[rows, :], near[...]).astype(BF16)
    acc[...] += product(near[...], xt[...], TN)


def kernel(
    mask, irrep, amps_hbm, f_hbm, out,
    amps, fin, sbuf, fm, ktile, gtile, kslot, gslot, dvec, dcol, dall, block, nt, u0, u3, u1, xt, acc,
    send_a, recv_a, send_b, recv_b,
    in_sem, f_send, f_recv, own_sem, k_sem, g_send, g_recv, d_send, d_recv, e_send, e_recv, b_send, b_recv,
    z_send, z_recv, y_send, y_recv, s_send, s_recv, sa, ra, sb, rb,
):
    row = lax.axis_index("row")
    col = lax.axis_index("col")
    half = row % 2
    chip = row // 2
    zhi = col // 4
    yat = col % 4
    sibling = row + 1 - 2 * half

    def remote(src, dst, send, recv, dest):
        return pltpu.make_async_remote_copy(
            src_ref=src, dst_ref=dst, send_sem=send, recv_sem=recv, device_id=dest, device_id_type=MESH
        )

    loads = [pltpu.make_async_copy(amps_hbm, amps, in_sem.at[3])]
    for g in range(3):
        loads.append(pltpu.make_async_copy(f_hbm.at[pl.ds(64 * g, 64)], fin.at[pl.ds(64 * g, 64)], in_sem.at[g]))
    for load in loads:
        load.start()

    barrier = pltpu.get_barrier_semaphore()

    def greet(peer):
        pl.semaphore_signal(barrier, inc=1, device_id=peer, device_id_type=MESH)

    for o in range(1, 16):
        greet(((row + o) % 16, col))
        greet((row, (col + o) % 16))
    for s in range(2):
        @pl.when(2 * chip + s != col)
        def _():
            greet((col, 2 * chip + s))

    loads[0].wait()
    own_tiles(mask, irrep, amps, ktile, gtile, dvec, row, col)
    for s in range(2):
        @pl.when(2 * chip + s == col)
        def _():
            gslot[s] = jnp.zeros((32, 128), BF16)

    pl.semaphore_wait(barrier, jnp.where(row == col, 30, 32))

    k_copy = remote(ktile.at[1 - half], kslot, k_sem.at[0], k_sem.at[1], (sibling, col))
    k_copy.start()
    g_copies = [
        remote(gtile.at[h], gslot.at[col % 2], g_send.at[h], g_recv.at[col % 2], (2 * (col // 2) + h, row))
        for h in range(2)
    ]
    d_copies = [remote(dvec, dcol, d_send.at[o], d_recv, (row, (row + o) % 16)) for o in range(1, 16)]

    @pl.when(row != col)
    def _():
        for copy in g_copies:
            copy.start()

    @pl.when(row == col)
    def _():
        dcol[...] = dvec[...]
        for copy in d_copies:
            copy.start()

    swap = row_swap()
    f_copies = [[], [], []]

    def send_factors(g):
        loads[1 + g].wait()
        regroup(fin, sbuf, g, swap)
        own = pltpu.make_async_copy(sbuf.at[g, row], fm.at[g, pl.ds(pl.multiple_of(64 * row, 64), 64)], own_sem.at[g])
        own.start()
        for o in range(1, 16):
            dest = (row + o) % 16
            copy = remote(
                sbuf.at[g, dest], fm.at[g, pl.ds(pl.multiple_of(64 * row, 64), 64)],
                f_send.at[g, o], f_recv.at[g, o], (dest, col),
            )
            copy.start()
            f_copies[g].append(copy)
        f_copies[g].append(own)

    send_factors(0)

    k_copy.wait_recv()
    for s in range(2):
        @pl.when(2 * chip + s != col)
        def _():
            remote(gtile.at[s], gslot.at[s], g_send.at[s], g_recv.at[s], (sibling, col)).wait_recv()
    summed = ktile[half].astype(F32) + kslot[...].astype(F32) + gslot[0].astype(F32) + gslot[1].astype(F32)
    block[...] = summed.astype(BF16)
    lanes = pl.ds(pl.multiple_of(128 * chip, 128), 128)
    mine = 2 * col + half
    nt[mine, :, lanes] = block[...]
    b_copies = []
    for o in range(1, 8):
        copy = remote(
            block, nt.at[mine, :, lanes], b_send.at[o], b_recv.at[o], (2 * ((chip + o) % 8) + half, col)
        )
        copy.start()
        b_copies.append(copy)

    @pl.when(row != col)
    def _():
        d_copies[0].wait_recv()

    dall[row] = dcol[...]
    e_copies = []
    for o in range(1, 16):
        copy = remote(dcol, dall.at[row], e_send.at[o], e_recv.at[o], ((row + o) % 16, col))
        copy.start()
        e_copies.append(copy)

    send_factors(1)

    for copy in b_copies:
        copy.wait_recv()

    m_copies = []

    def to_y(k, piece):
        for o in range(1, 4):
            copy = remote(
                nt.at[piece], nt.at[piece], y_send.at[k, o], y_recv.at[k, o], (row, 4 * zhi + (yat + o) % 4)
            )
            copy.start()
            m_copies.append(copy)

    def to_sibling(at, piece):
        copy = remote(nt.at[piece], nt.at[piece], s_send.at[at], s_recv.at[at], (sibling, col))
        copy.start()
        m_copies.append(copy)

    z_copies = []
    for o in range(1, 4):
        copy = remote(
            nt.at[mine], nt.at[mine], z_send.at[o], z_recv.at[o], (row, 4 * ((zhi + o) % 4) + yat)
        )
        copy.start()
        z_copies.append(copy)
    to_y(0, mine)
    to_sibling(0, mine)

    send_factors(2)

    for k in range(1, 4):
        z_copies[k - 1].wait_recv()
        piece = 2 * (4 * ((zhi + 4 - k) % 4) + yat) + half
        to_y(k, piece)
        to_sibling(4 * k, piece)
    for k in range(4):
        for o in range(1, 4):
            piece = 2 * (4 * ((zhi + 4 - k) % 4) + (yat + 4 - o) % 4) + half
            remote(
                nt.at[piece], nt.at[piece], y_send.at[k, o], y_recv.at[k, o], (sibling, col)
            ).wait_recv()
            to_sibling(4 * k + o, piece)
    for copy in e_copies:
        copy.wait_recv()
    for at in range(16):
        k, o = at // 4, at % 4
        piece = 2 * (4 * ((zhi + 4 - k) % 4) + (yat + 4 - o) % 4) + 1 - half
        remote(nt.at[piece], nt.at[piece], s_send.at[at], s_recv.at[at], (sibling, col)).wait_recv()

    split_matrix(irrep, nt, dall, u0, u3, u1)
    acc[...] = jnp.zeros_like(acc)
    for g in range(3):
        for copy in f_copies[g][:15]:
            copy.wait_recv()
        f_copies[g][15].wait()
        chunk_sums(fm.at[g], u0, u3, u1, xt, acc)

    sums = []
    for p in range(3):
        total = jnp.zeros((64, 64), F32)
        for k in range(4):
            total = total + acc[64 * k : 64 * k + 64, 256 * p + 64 * k : 256 * p + 64 * k + 64]
        sums.append(total)
    near = (sums[0] + sums[0].T, sums[2].T, sums[2], sums[1] + sums[1].T)
    for r in range(16):
        for p in range(4):
            send_a[r, 4 * p : 4 * p + 4, :] = near[p][4 * r : 4 * r + 4, :]
    a_copies = []
    for o in range(1, 16):
        dest = (row + o) % 16
        copy = remote(send_a.at[dest], recv_a.at[o], sa.at[o], ra.at[o], (dest, col))
        copy.start()
        a_copies.append(copy)
    total = send_a[row]
    for o in range(1, 16):
        a_copies[o - 1].wait_recv()
        total = total + recv_a[o]
    turned = total.T
    for c in range(16):
        send_b[c] = turned[4 * c : 4 * c + 4, :]
    c_copies = []
    for o in range(1, 16):
        dest = (col + o) % 16
        copy = remote(send_b.at[dest], recv_b.at[o], sb.at[o], rb.at[o], (row, dest))
        copy.start()
        c_copies.append(copy)
    final = send_b[col]
    for o in range(1, 16):
        c_copies[o - 1].wait_recv()
        final = final + recv_b[o]
    back = final.T
    for p in range(4):
        out[p] = back[4 * p : 4 * p + 4, :]

    k_copy.wait_send()

    @pl.when(row != col)
    def _():
        for copy in g_copies:
            copy.wait_send()

    @pl.when(row == col)
    def _():
        for copy in d_copies:
            copy.wait_send()

    for copies in (f_copies[0][:15], f_copies[1][:15], f_copies[2][:15], b_copies, e_copies, z_copies, m_copies,
                   a_copies, c_copies):
        for copy in copies:
            copy.wait_send()


def per_device(amplitudes, factors, tile_mask, tile_irrep):
    smem = pl.BlockSpec(memory_space=pltpu.SMEM)
    place = pl.BlockSpec(memory_space=pl.ANY)
    dma = pltpu.SemaphoreType.DMA
    return pl.pallas_call(
        kernel,
        out_shape=jax.ShapeDtypeStruct((4, 4, 4), F32),
        in_specs=[smem, smem, place, place],
        out_specs=pl.BlockSpec(memory_space=pltpu.VMEM),
        scratch_shapes=[
            pltpu.VMEM((4, 64, 64), BF16),
            pltpu.VMEM((192, 4096), BF16),
            pltpu.VMEM((3, 16, 64, 256), BF16),
            pltpu.VMEM((3, 1024, 256), BF16),
            pltpu.VMEM((2, 32, 128), BF16),
            pltpu.VMEM((2, 32, 128), BF16),
            pltpu.VMEM((32, 128), BF16),
            pltpu.VMEM((2, 32, 128), BF16),
            pltpu.VMEM((8, 128), BF16),
            pltpu.VMEM((8, 128), BF16),
            pltpu.VMEM((16, 8, 128), BF16),
            pltpu.VMEM((32, 128), BF16),
            pltpu.VMEM((32, 32, 1024), BF16),
            pltpu.VMEM((1024, 1024), BF16),
            pltpu.VMEM((1024, 1024), BF16),
            pltpu.VMEM((1024, 1024), BF16),
            pltpu.VMEM((1024, 768), BF16),
            pltpu.VMEM((256, 768), F32),
            pltpu.VMEM((16, 16, 64), F32),
            pltpu.VMEM((16, 16, 64), F32),
            pltpu.VMEM((16, 4, 16), F32),
            pltpu.VMEM((16, 4, 16), F32),
            dma((4,)), dma((3, 16)), dma((3, 16)), dma((3,)), dma((2,)), dma((2,)), dma((2,)),
            dma((16,)), dma(()), dma((16,)), dma((16,)), dma((8,)), dma((8,)),
            dma((4,)), dma((4,)), dma((4, 4)), dma((4, 4)), dma((16,)), dma((16,)),
            dma((16,)), dma((16,)), dma((16,)), dma((16,)),
        ],
        compiler_params=pltpu.CompilerParams(collective_id=0, has_side_effects=True, vmem_limit_bytes=48 << 20),
        name="ladder",
    )(tile_mask, tile_irrep, amplitudes, factors)


def solution(mesh):
    return jax.shard_map(
        per_device,
        mesh=mesh,
        in_specs=(P(None, "row", "col"), P("col", "row"), P(), P()),
        out_specs=P(None, "row", "col"),
        check_vma=False,
    )
```

```python
import jax
import jax.numpy as jnp
from jax import lax
from jax.experimental import pallas as pl
from jax.experimental.pallas import tpu as pltpu
from jax.sharding import PartitionSpec as P

MESH = pl.DeviceIdType.MESH
F32 = jnp.float32
BF16 = jnp.bfloat16
NN = (((1,), (0,)), ((), ()))
NT_DIMS = (((1,), (1,)), ((), ()))
TN = (((0,), (0,)), ((), ()))


def product(left, right, dims=NN):
    return lax.dot_general(left, right, dims, preferred_element_type=F32)


def row_swap():
    at = lax.broadcasted_iota(jnp.int32, (256, 256), 0)
    come = lax.broadcasted_iota(jnp.int32, (256, 256), 1)
    hit = (at // 16 == come % 16) & (at % 16 == come // 16)
    return jnp.where(hit, 1.0, 0.0).astype(BF16)


def regroup(fin, sbuf, g, swap):
    low = lax.broadcasted_iota(jnp.int32, (16, 128), 1) < 64
    for jb in range(2):
        stacks = ([], [])
        for jj in range(16):
            cols = pl.ds(128 * (16 * jb + jj), 128)
            halves = ([], [])
            for kp in range(2):
                v0 = fin[pl.ds(64 * g + 32 * kp, 16), cols].astype(F32)
                v1 = fin[pl.ds(64 * g + 32 * kp + 16, 16), cols].astype(F32)
                halves[0].append(jnp.where(low, v0, pltpu.roll(v1, 64, 1)).astype(BF16))
                halves[1].append(jnp.where(low, pltpu.roll(v0, 64, 1), v1).astype(BF16))
            for e in range(2):
                stacks[e].append(jnp.concatenate(halves[e], axis=1))
        for e in range(2):
            moved = product(swap, jnp.concatenate(stacks[e], axis=0)).astype(BF16)
            for r in range(16):
                sbuf[r, g, pl.ds(32 * e + 16 * jb, 16), :] = moved[16 * r : 16 * r + 16, :]


def unpacked(ref, side):
    low = lax.broadcasted_iota(jnp.int32, (16, 128), 1) < 64
    packed = ref[...].astype(F32)
    turned = pltpu.roll(packed, 64, 1)
    rows = jnp.concatenate([jnp.where(low, packed, turned), jnp.where(low, turned, packed)], axis=0)
    lane = lax.broadcasted_iota(jnp.int32, (32, 128), 1)
    return jnp.where(lane // 64 == side, rows, 0.0)


def own_tiles(mask, irrep, amps, kfull, ktile, gtile, dvec, row, col):
    at = lax.broadcasted_iota(jnp.int32, (64, 64), 0)
    to = lax.broadcasted_iota(jnp.int32, (64, 64), 1)
    left = jnp.where(to == 2 * (at % 32) + at // 32, 1.0, 0.0).astype(BF16)
    at = lax.broadcasted_iota(jnp.int32, (64, 128), 0)
    to = lax.broadcasted_iota(jnp.int32, (64, 128), 1)
    within = to % 64
    right = jnp.where(at == 2 * (within % 32) + within // 32, 1.0, 0.0).astype(BF16)
    crossed = jnp.abs(irrep[row].astype(F32) - irrep[col].astype(F32))
    stored = mask[row, col].astype(F32)
    alike = stored * (1.0 - crossed)
    unlike = stored * crossed
    upper = (row <= col).astype(F32)
    lower = 1.0 - upper
    a0, a1, a2, a3 = (amps[p].astype(F32) for p in range(4))
    kept = ((alike * upper) * a0 + (alike * lower) * a3 + unlike * a1).astype(BF16)
    given = ((alike * upper) * a3 + (alike * lower) * a0 + unlike * a2).astype(BF16)
    kept_turned = product(product(left, kept, NT_DIMS).astype(BF16), right)
    kept_plain = product(product(left, kept).astype(BF16), right)
    given_turned = product(product(left, given, NT_DIMS).astype(BF16), right)
    given_plain = product(product(left, given).astype(BF16), right)
    both = jnp.where(
        within < at, kept_turned + kept_plain, jnp.where(within > at, given_turned + given_plain, kept_plain)
    )
    on_diagonal = (row == col).astype(F32)
    mine = on_diagonal * both + (1.0 - on_diagonal) * kept_turned
    low = lax.broadcasted_iota(jnp.int32, (16, 128), 1) < 64
    for h in range(2):
        at_h = 32 * h
        kfull[h] = jnp.where(to[:32] // 64 == row % 2, mine[at_h : at_h + 32], 0.0)
        ktile[h] = jnp.where(low, mine[at_h : at_h + 16], mine[at_h + 16 : at_h + 32]).astype(BF16)
        gtile[h] = jnp.where(low, given_plain[at_h : at_h + 16], given_plain[at_h + 16 : at_h + 32]).astype(BF16)
    line = jnp.sum(jnp.where(to == at, given_plain, 0.0), axis=1, keepdims=True)
    dvec[...] = jnp.broadcast_to(line, (64, 128)).astype(BF16)


def lane_irreps(irrep):
    lane = lax.broadcasted_iota(jnp.int32, (1, 1024), 1)
    out = jnp.zeros((1, 1024), F32)
    for t in range(16):
        out = jnp.where(lane // 64 == t, irrep[t].astype(F32), out)
    return out


def split_rows(i, chip, irrep, of_lane, nt, u0, u3, u1):
    bits = (chip // 4, chip // 2 % 2, chip % 2)
    place = []
    for j in range(8):
        offsets = [1 - bit if (j >> (2 - n)) & 1 else bit for n, bit in enumerate(bits)]
        place.append(4 * offsets[0] + 2 * offsets[1] + offsets[2])
    lane2 = lax.broadcasted_iota(jnp.int32, (64, 128), 1)
    row2 = lax.broadcasted_iota(jnp.int32, (64, 128), 0)
    for y in range(4):
        t = 4 * i + y
        differs = jnp.abs(of_lane - irrep[t].astype(F32))
        same = 1.0 - differs
        offset = lane2 - 64 * (t % 2)
        in_tile = (offset >= 0) & (offset < 64)
        here = jnp.broadcast_to(same[:, 128 * (t // 2) : 128 * (t // 2) + 128], (64, 128))
        here0 = jnp.where((offset < 0) | (in_tile & (offset <= row2)), here, 0.0).astype(BF16)
        here3 = jnp.where((offset >= 64) | (in_tile & (offset > row2)), here, 0.0).astype(BF16)
        alike = same.astype(BF16)
        unlike = differs.astype(BF16)
        for h in range(2):
            rows = pl.ds(64 * t + 32 * h, 32)
            sub = slice(32 * h, 32 * h + 32)
            for j in range(8):
                lanes = slice(128 * j, 128 * j + 128)
                tile = nt[h, y, place[j], i]
                u1[rows, lanes] = tile * unlike[:, lanes]
                if j == t // 2:
                    u0[rows, lanes] = tile * here0[sub]
                    u3[rows, lanes] = tile * here3[sub]
                elif j < t // 2:
                    u0[rows, lanes] = tile * alike[:, lanes]
                    if j >= 2 * i:
                        u3[rows, lanes] = jnp.zeros((32, 128), BF16)
                else:
                    u3[rows, lanes] = tile * alike[:, lanes]
                    if j < 2 * i + 2:
                        u0[rows, lanes] = jnp.zeros((32, 128), BF16)


def row_sums(i, near, u0, u3, u1, acc):
    rows = pl.ds(256 * i, 256)
    done = 256 * (i + 1)
    x0 = product(u0[rows, :done], near[:done, :]).astype(BF16)
    x3 = product(u3[rows, 256 * i :], near[256 * i :, :]).astype(BF16)
    x1 = product(u1[rows, :], near[...]).astype(BF16)
    acc[...] += product(near[rows, :], jnp.concatenate([x0, x3, x1], axis=1), TN)


def kernel(
    mask_hbm, irrep_hbm, amps_hbm, f_hbm, out,
    mask, irrep, amps, fin, sbuf, fm, kfull, ktile, gtile, kslot, gslot, dvec, dcol, nt, u0, u3, u1, acc,
    send_a, recv_a, send_b, recv_b,
    in_sem, f_send, f_recv, own_sem, k_sem, g_send, g_recv, d_send, d_recv, b_send, b_recv,
    z_send, z_recv, y_send, y_recv, s_send, s_recv, sa, ra, sb, rb,
):
    row = lax.axis_index("row")
    col = lax.axis_index("col")
    half = row % 2
    chip = row // 2
    zhi = col // 4
    yat = col % 4
    sibling = row + 1 - 2 * half

    def remote(src, dst, send, recv, dest):
        return pltpu.make_async_remote_copy(
            src_ref=src, dst_ref=dst, send_sem=send, recv_sem=recv, device_id=dest, device_id_type=MESH
        )

    loads = [
        pltpu.make_async_copy(amps_hbm, amps, in_sem.at[3]),
        pltpu.make_async_copy(mask_hbm, mask, in_sem.at[4]),
        pltpu.make_async_copy(irrep_hbm, irrep, in_sem.at[5]),
    ]
    for g in range(3):
        loads.append(pltpu.make_async_copy(f_hbm.at[pl.ds(64 * g, 64)], fin.at[pl.ds(64 * g, 64)], in_sem.at[g]))
    for load in loads:
        load.start()

    barrier = pltpu.get_barrier_semaphore()

    def greet(peer):
        pl.semaphore_signal(barrier, inc=1, device_id=peer, device_id_type=MESH)

    for o in range(1, 16):
        greet(((row + o) % 16, col))
        greet((row, (col + o) % 16))
    for s in range(2):
        @pl.when(2 * chip + s != col)
        def _():
            greet((col, 2 * chip + s))

    for load in loads[:3]:
        load.wait()
    own_tiles(mask, irrep, amps, kfull, ktile, gtile, dvec, row, col)
    for s in range(2):
        @pl.when(2 * chip + s == col)
        def _():
            gslot[s] = jnp.zeros((16, 128), BF16)
    pl.semaphore_wait(barrier, jnp.where(row == col, 30, 32))

    k_copy = remote(ktile.at[1 - half], kslot, k_sem.at[0], k_sem.at[1], (sibling, col))
    k_copy.start()
    g_copies = [
        remote(gtile.at[h], gslot.at[col % 2], g_send.at[h], g_recv.at[col % 2], (2 * (col // 2) + h, row))
        for h in range(2)
    ]
    d_copies = [remote(dvec, dcol, d_send.at[o], d_recv, (row, (row + o) % 16)) for o in range(1, 16)]

    @pl.when(row != col)
    def _():
        for copy in g_copies:
            copy.start()

    swap = row_swap()
    f_copies = [[], [], []]

    def send_factors(part):
        first, count = part, 1
        for g in range(first, first + count):
            loads[3 + g].wait()
            regroup(fin, sbuf, g, swap)
        groups = pl.ds(first, count)
        place = pl.ds(pl.multiple_of(64 * row, 64), 64)
        for o in range(1, 16):
            dest = (row + o) % 16
            copy = remote(
                sbuf.at[dest, groups], fm.at[groups, place], f_send.at[part, o], f_recv.at[part, o], (dest, col)
            )
            copy.start()
            f_copies[part].append(copy)
        copy = pltpu.make_async_copy(sbuf.at[row, groups], fm.at[groups, place], own_sem.at[part])
        copy.start()
        f_copies[part].append(copy)

    send_factors(0)
    of_lane = lane_irreps(irrep)
    acc[...] = jnp.zeros_like(acc)

    k_copy.wait_recv()
    for s in range(2):
        @pl.when(2 * chip + s != col)
        def _():
            remote(gtile.at[s], gslot.at[s], g_send.at[s], g_recv.at[s], (sibling, col)).wait_recv()
    summed = kfull[half] + unpacked(kslot, 1 - half) + unpacked(gslot.at[0], 0) + unpacked(gslot.at[1], 1)
    nt[half, yat, 0, zhi] = summed.astype(BF16)
    z_copies = []
    for o in range(1, 4):
        at = nt.at[half, yat, 0, zhi]
        copy = remote(at, at, z_send.at[o], z_recv.at[o], (row, 4 * ((zhi + o) % 4) + yat))
        copy.start()
        z_copies.append(copy)

    @pl.when(row == col)
    def _():
        dcol[...] = dvec[...]
        for copy in d_copies:
            copy.start()


    for o in range(1, 4):
        at = nt.at[half, yat, 0, (zhi + 4 - o) % 4]
        remote(at, at, z_send.at[o], z_recv.at[o], (sibling, col)).wait_recv()
    xhigh, xlow, zlo = chip // 4, chip // 2 % 2, chip % 2

    def flipped(bit, by):
        return 1 - bit if by else bit

    def at_offset(m):
        return 4 * flipped(xhigh, m // 4) + 2 * flipped(xlow, m // 2 % 2) + flipped(zlo, m % 2)

    b_copies = []
    for m in range(1, 8):
        copy = remote(
            nt.at[half, yat, 0], nt.at[half, yat, m], b_send.at[m], b_recv.at[m], (2 * at_offset(m) + half, col)
        )
        copy.start()
        b_copies.append(copy)

    def piece(h, y, p):
        return nt.at[h, y, p] if p < 2 else nt.at[h, y, pl.ds(2, 6), p - 2]

    y_copies = []
    m_copies = []

    def send_piece(p):
        at = piece(half, yat, p)
        copies = [
            remote(at, at, y_send.at[p, o], y_recv.at[p, o], (row, 4 * zhi + (yat + o) % 4)) for o in range(1, 4)
        ]
        copies.append(remote(at, at, s_send.at[p, 0], s_recv.at[p, 0], (sibling, col)))
        for copy in copies:
            copy.start()
        y_copies.append(copies)

    def take_pieces(pieces):
        for p in pieces:
            for o in range(1, 4):
                at = piece(half, (yat + 4 - o) % 4, p)
                remote(at, at, y_send.at[p, o], y_recv.at[p, o], (sibling, col)).wait_recv()
                copy = remote(at, at, s_send.at[p, o], s_recv.at[p, o], (sibling, col))
                copy.start()
                m_copies.append(copy)
        for p in pieces:
            for o in range(4):
                at = piece(1 - half, (yat + 4 - o) % 4, p)
                remote(at, at, s_send.at[p, o], s_recv.at[p, o], (sibling, col)).wait_recv()

    def factors_here(part):
        f_copies[part][15].wait()
        for copy in f_copies[part][:15]:
            copy.wait_recv()

    send_piece(0)
    b_copies[0].wait_recv()
    send_piece(1)
    send_factors(1)
    for copy in b_copies[1:]:
        copy.wait_recv()
    send_piece(2)
    send_piece(3)
    send_factors(2)

    @pl.when(row != col)
    def _():
        d_copies[0].wait_recv()

    scale = jnp.concatenate([dcol[...], dcol[...]], axis=1)
    diagonal = jnp.zeros((256, 256), F32)
    for g in range(3):
        plain = jnp.concatenate([sbuf[r, g] for r in range(16)], axis=0)
        scaled = jnp.concatenate([sbuf[r, g] * scale for r in range(16)], axis=0)
        diagonal = diagonal + product(scaled, plain, TN)
    acc[:, 256:512] = diagonal

    plan = (
        ((0, 0),),
        ((1, 0), (0, 1), (1, 1)),
        ((2, 0), (2, 1)),
        ((3, 0), (3, 1), (0, 2), (1, 2), (2, 2), (3, 2)),
    )
    arrived = set()
    for i in range(4):
        if i < 2:
            for copy in y_copies[2 + i]:
                copy.wait_send()
            send_piece(4 + i)
        take_pieces((0, 1, 2) if i == 0 else (2 + i,))
        split_rows(i, chip, irrep, of_lane, nt, u0, u3, u1)
        for k, g in plan[i]:
            if g not in arrived:
                arrived.add(g)
                factors_here(g)
            row_sums(k, fm.at[g], u0, u3, u1, acc)
    for p in (0, 1, 4, 5):
        m_copies += y_copies[p]

    sums = []
    for p in range(3):
        total = jnp.zeros((64, 64), F32)
        for k in range(4):
            total = total + acc[64 * k : 64 * k + 64, 256 * p + 64 * k : 256 * p + 64 * k + 64]
        sums.append(total)
    near = (sums[0] + sums[0].T, sums[2].T, sums[2], sums[1] + sums[1].T)
    for r in range(16):
        for p in range(4):
            send_a[r, 4 * p : 4 * p + 4, :] = near[p][4 * r : 4 * r + 4, :]
    a_copies = []
    for o in range(1, 16):
        dest = (row + o) % 16
        copy = remote(send_a.at[dest], recv_a.at[o], sa.at[o], ra.at[o], (dest, col))
        copy.start()
        a_copies.append(copy)
    total = send_a[row]
    for o in range(1, 16):
        a_copies[o - 1].wait_recv()
        total = total + recv_a[o]
    turned = total.T
    for c in range(16):
        send_b[c] = turned[4 * c : 4 * c + 4, :]
    c_copies = []
    for o in range(1, 16):
        dest = (col + o) % 16
        copy = remote(send_b.at[dest], recv_b.at[o], sb.at[o], rb.at[o], (row, dest))
        copy.start()
        c_copies.append(copy)
    final = send_b[col]
    for o in range(1, 16):
        c_copies[o - 1].wait_recv()
        final = final + recv_b[o]
    back = final.T
    for p in range(4):
        out[p] = back[4 * p : 4 * p + 4, :]

    k_copy.wait_send()

    @pl.when(row != col)
    def _():
        for copy in g_copies:
            copy.wait_send()

    @pl.when(row == col)
    def _():
        for copy in d_copies:
            copy.wait_send()

    for copies in (f_copies[0][:15], f_copies[1][:15], f_copies[2][:15], b_copies, z_copies, m_copies,
                   a_copies, c_copies):
        for copy in copies:
            copy.wait_send()


def per_device(amplitudes, factors, tile_mask, tile_irrep):
    place = pl.BlockSpec(memory_space=pltpu.HBM)
    dma = pltpu.SemaphoreType.DMA
    return pl.pallas_call(
        kernel,
        out_shape=jax.ShapeDtypeStruct((4, 4, 4), F32),
        in_specs=[place] * 4,
        out_specs=pl.BlockSpec(memory_space=pltpu.VMEM),
        scratch_shapes=[
            pltpu.SMEM((16, 16), jnp.int32),
            pltpu.SMEM((16,), jnp.int32),
            pltpu.VMEM((4, 64, 64), BF16),
            pltpu.VMEM((192, 4096), BF16),
            pltpu.VMEM((16, 3, 64, 256), BF16),
            pltpu.VMEM((3, 1024, 256), BF16),
            pltpu.VMEM((2, 32, 128), F32),
            pltpu.VMEM((2, 16, 128), BF16),
            pltpu.VMEM((2, 16, 128), BF16),
            pltpu.VMEM((16, 128), BF16),
            pltpu.VMEM((2, 16, 128), BF16),
            pltpu.VMEM((64, 128), BF16),
            pltpu.VMEM((64, 128), BF16),
            pltpu.VMEM((2, 4, 8, 4, 32, 128), BF16),
            pltpu.VMEM((1024, 1024), BF16),
            pltpu.VMEM((1024, 1024), BF16),
            pltpu.VMEM((1024, 1024), BF16),
            pltpu.VMEM((256, 768), F32),
            pltpu.VMEM((16, 16, 64), F32),
            pltpu.VMEM((16, 16, 64), F32),
            pltpu.VMEM((16, 4, 16), F32),
            pltpu.VMEM((16, 4, 16), F32),
            dma((6,)), dma((3, 16)), dma((3, 16)), dma((3,)), dma((2,)), dma((2,)), dma((2,)),
            dma((16,)), dma(()), dma((8,)), dma((8,)),
            dma((4,)), dma((4,)), dma((6, 4)), dma((6, 4)), dma((6, 4)), dma((6, 4)),
            dma((16,)), dma((16,)), dma((16,)), dma((16,)),
        ],
        compiler_params=pltpu.CompilerParams(collective_id=0, has_side_effects=True, vmem_limit_bytes=62 << 20),
        name="ladder",
    )(tile_mask, tile_irrep, amplitudes, factors)


def solution(mesh):
    return jax.shard_map(
        per_device,
        mesh=mesh,
        in_specs=(P(None, "row", "col"), P("col", "row"), P(), P()),
        out_specs=P(None, "row", "col"),
        check_vma=False,
    )
```

```python
import jax
import jax.numpy as jnp
from jax import lax
from jax.experimental import pallas as pl
from jax.experimental.pallas import tpu as pltpu
from jax.sharding import PartitionSpec as P

MESH = pl.DeviceIdType.MESH
F32 = jnp.float32
BF16 = jnp.bfloat16
NN = (((1,), (0,)), ((), ()))
NT_DIMS = (((1,), (1,)), ((), ()))
TN = (((0,), (0,)), ((), ()))


def product(left, right, dims=NN):
    return lax.dot_general(left, right, dims, preferred_element_type=F32)


def row_swap():
    at = lax.broadcasted_iota(jnp.int32, (256, 256), 0)
    come = lax.broadcasted_iota(jnp.int32, (256, 256), 1)
    hit = (at // 16 == come % 16) & (at % 16 == come // 16)
    return jnp.where(hit, 1.0, 0.0).astype(BF16)


def regroup(fin, sbuf, g, swap):
    low = lax.broadcasted_iota(jnp.int32, (16, 128), 1) < 64
    for jb in range(2):
        stacks = ([], [])
        for jj in range(16):
            cols = pl.ds(128 * (16 * jb + jj), 128)
            halves = ([], [])
            for kp in range(2):
                v0 = fin[pl.ds(64 * g + 32 * kp, 16), cols].astype(F32)
                v1 = fin[pl.ds(64 * g + 32 * kp + 16, 16), cols].astype(F32)
                halves[0].append(jnp.where(low, v0, pltpu.roll(v1, 64, 1)).astype(BF16))
                halves[1].append(jnp.where(low, pltpu.roll(v0, 64, 1), v1).astype(BF16))
            for e in range(2):
                stacks[e].append(jnp.concatenate(halves[e], axis=1))
        for e in range(2):
            moved = product(swap, jnp.concatenate(stacks[e], axis=0)).astype(BF16)
            for r in range(16):
                sbuf[r, g, pl.ds(32 * e + 16 * jb, 16), :] = moved[16 * r : 16 * r + 16, :]


def unpacked(ref, side):
    low = lax.broadcasted_iota(jnp.int32, (16, 128), 1) < 64
    packed = ref[...].astype(F32)
    turned = pltpu.roll(packed, 64, 1)
    rows = jnp.concatenate([jnp.where(low, packed, turned), jnp.where(low, turned, packed)], axis=0)
    lane = lax.broadcasted_iota(jnp.int32, (32, 128), 1)
    return jnp.where(lane // 64 == side, rows, 0.0)


def own_tiles(mask, irrep, amps, kfull, ktile, gtile, dvec, row, col):
    at = lax.broadcasted_iota(jnp.int32, (64, 64), 0)
    to = lax.broadcasted_iota(jnp.int32, (64, 64), 1)
    left = jnp.where(to == 2 * (at % 32) + at // 32, 1.0, 0.0).astype(BF16)
    at = lax.broadcasted_iota(jnp.int32, (64, 128), 0)
    to = lax.broadcasted_iota(jnp.int32, (64, 128), 1)
    within = to % 64
    right = jnp.where(at == 2 * (within % 32) + within // 32, 1.0, 0.0).astype(BF16)
    crossed = jnp.abs(irrep[row].astype(F32) - irrep[col].astype(F32))
    stored = mask[row, col].astype(F32)
    alike = stored * (1.0 - crossed)
    unlike = stored * crossed
    upper = (row <= col).astype(F32)
    lower = 1.0 - upper
    a0, a1, a2, a3 = (amps[p].astype(F32) for p in range(4))
    kept = ((alike * upper) * a0 + (alike * lower) * a3 + unlike * a1).astype(BF16)
    given = ((alike * upper) * a3 + (alike * lower) * a0 + unlike * a2).astype(BF16)
    kept_turned = product(product(left, kept, NT_DIMS).astype(BF16), right)
    kept_plain = product(product(left, kept).astype(BF16), right)
    given_turned = product(product(left, given, NT_DIMS).astype(BF16), right)
    given_plain = product(product(left, given).astype(BF16), right)
    both = jnp.where(
        within < at, kept_turned + kept_plain, jnp.where(within > at, given_turned + given_plain, kept_plain)
    )
    on_diagonal = (row == col).astype(F32)
    mine = on_diagonal * both + (1.0 - on_diagonal) * kept_turned
    low = lax.broadcasted_iota(jnp.int32, (16, 128), 1) < 64
    for h in range(2):
        at_h = 32 * h
        kfull[h] = jnp.where(to[:32] // 64 == row % 2, mine[at_h : at_h + 32], 0.0)
        ktile[h] = jnp.where(low, mine[at_h : at_h + 16], mine[at_h + 16 : at_h + 32]).astype(BF16)
        gtile[h] = jnp.where(low, given_plain[at_h : at_h + 16], given_plain[at_h + 16 : at_h + 32]).astype(BF16)
    line = jnp.sum(jnp.where(to == at, given_plain, 0.0), axis=1, keepdims=True)
    dvec[...] = jnp.broadcast_to(line, (64, 128)).astype(BF16)


def lane_irreps(irrep):
    lane = lax.broadcasted_iota(jnp.int32, (1, 1024), 1)
    out = jnp.zeros((1, 1024), F32)
    for t in range(16):
        out = jnp.where(lane // 64 == t, irrep[t].astype(F32), out)
    return out


def split_rows(i, chip, irrep, of_lane, nt, u0, u3, u1):
    bits = (chip // 4, chip // 2 % 2, chip % 2)
    place = []
    for j in range(8):
        offsets = [1 - bit if (j >> (2 - n)) & 1 else bit for n, bit in enumerate(bits)]
        place.append(4 * offsets[0] + 2 * offsets[1] + offsets[2])
    lane2 = lax.broadcasted_iota(jnp.int32, (64, 128), 1)
    row2 = lax.broadcasted_iota(jnp.int32, (64, 128), 0)
    for y in range(4):
        t = 4 * i + y
        differs = jnp.abs(of_lane - irrep[t].astype(F32))
        same = 1.0 - differs
        offset = lane2 - 64 * (t % 2)
        in_tile = (offset >= 0) & (offset < 64)
        here = jnp.broadcast_to(same[:, 128 * (t // 2) : 128 * (t // 2) + 128], (64, 128))
        here0 = jnp.where((offset < 0) | (in_tile & (offset <= row2)), here, 0.0).astype(BF16)
        here3 = jnp.where((offset >= 64) | (in_tile & (offset > row2)), here, 0.0).astype(BF16)
        alike = same.astype(BF16)
        unlike = differs.astype(BF16)
        for h in range(2):
            rows = pl.ds(64 * t + 32 * h, 32)
            sub = slice(32 * h, 32 * h + 32)
            for j in range(8):
                lanes = slice(128 * j, 128 * j + 128)
                tile = nt[h, y, place[j], i]
                u1[rows, lanes] = tile * unlike[:, lanes]
                if j == t // 2:
                    u0[rows, lanes] = tile * here0[sub]
                    u3[rows, lanes] = tile * here3[sub]
                elif j < t // 2:
                    u0[rows, lanes] = tile * alike[:, lanes]
                    if j >= 2 * i:
                        u3[rows, lanes] = jnp.zeros((32, 128), BF16)
                else:
                    u3[rows, lanes] = tile * alike[:, lanes]
                    if j < 2 * i + 2:
                        u0[rows, lanes] = jnp.zeros((32, 128), BF16)


def row_sums(i, near, u0, u3, u1, acc):
    rows = pl.ds(256 * i, 256)
    done = 256 * (i + 1)
    x0 = product(u0[rows, :done], near[:done, :]).astype(BF16)
    x3 = product(u3[rows, 256 * i :], near[256 * i :, :]).astype(BF16)
    x1 = product(u1[rows, :], near[...]).astype(BF16)
    acc[...] += product(near[rows, :], jnp.concatenate([x0, x3, x1], axis=1), TN)


def kernel(
    mask_hbm, irrep_hbm, amps_hbm, f_hbm, out,
    mask, irrep, amps, fin, sbuf, fm, kfull, ktile, gtile, kslot, gslot, dvec, dcol, nt, u0, u3, u1, acc,
    send_a, recv_a, send_b, recv_b,
    in_sem, f_send, f_recv, own_sem, k_sem, g_send, g_recv, d_send, d_recv, b_send, b_recv,
    z_send, z_recv, y_send, y_recv, s_send, s_recv, sa, ra, sb, rb,
):
    row = lax.axis_index("row")
    col = lax.axis_index("col")
    half = row % 2
    chip = row // 2
    zhi = col // 4
    yat = col % 4
    sibling = row + 1 - 2 * half

    def remote(src, dst, send, recv, dest):
        return pltpu.make_async_remote_copy(
            src_ref=src, dst_ref=dst, send_sem=send, recv_sem=recv, device_id=dest, device_id_type=MESH
        )

    loads = [
        pltpu.make_async_copy(amps_hbm, amps, in_sem.at[3]),
        pltpu.make_async_copy(mask_hbm, mask, in_sem.at[4]),
        pltpu.make_async_copy(irrep_hbm, irrep, in_sem.at[5]),
    ]
    for g in range(3):
        loads.append(pltpu.make_async_copy(f_hbm.at[pl.ds(64 * g, 64)], fin.at[pl.ds(64 * g, 64)], in_sem.at[g]))
    for load in loads:
        load.start()

    barrier = pltpu.get_barrier_semaphore()

    def greet(peer):
        pl.semaphore_signal(barrier, inc=1, device_id=peer, device_id_type=MESH)

    for o in range(1, 16):
        greet(((row + o) % 16, col))
        greet((row, (col + o) % 16))
    for s in range(2):
        @pl.when(2 * chip + s != col)
        def _():
            greet((col, 2 * chip + s))

    for load in loads[:3]:
        load.wait()
    own_tiles(mask, irrep, amps, kfull, ktile, gtile, dvec, row, col)
    for s in range(2):
        @pl.when(2 * chip + s == col)
        def _():
            gslot[s] = jnp.zeros((16, 128), BF16)
    pl.semaphore_wait(barrier, jnp.where(row == col, 30, 32))

    k_copy = remote(ktile.at[1 - half], kslot, k_sem.at[0], k_sem.at[1], (sibling, col))
    k_copy.start()
    g_copies = [
        remote(gtile.at[h], gslot.at[col % 2], g_send.at[h], g_recv.at[col % 2], (2 * (col // 2) + h, row))
        for h in range(2)
    ]
    d_copies = [remote(dvec, dcol, d_send.at[o], d_recv, (row, (row + o) % 16)) for o in range(1, 16)]

    @pl.when(row != col)
    def _():
        for copy in g_copies:
            copy.start()

    swap = row_swap()
    f_copies = [[], [], []]

    def send_factors(part):
        first, count = part, 1
        groups = pl.ds(first, count)
        place = pl.ds(pl.multiple_of(64 * row, 64), 64)
        for o in range(1, 16):
            dest = (row + o) % 16
            copy = remote(
                sbuf.at[dest, groups], fm.at[groups, place], f_send.at[part, o], f_recv.at[part, o], (dest, col)
            )
            copy.start()
            f_copies[part].append(copy)
        copy = pltpu.make_async_copy(sbuf.at[row, groups], fm.at[groups, place], own_sem.at[part])
        copy.start()
        f_copies[part].append(copy)

    for part in range(3):
        loads[3 + part].wait()
        regroup(fin, sbuf, part, swap)
        if part == 0:
            send_factors(0)
    of_lane = lane_irreps(irrep)
    acc[...] = jnp.zeros_like(acc)

    k_copy.wait_recv()
    for s in range(2):
        @pl.when(2 * chip + s != col)
        def _():
            remote(gtile.at[s], gslot.at[s], g_send.at[s], g_recv.at[s], (sibling, col)).wait_recv()
    summed = kfull[half] + unpacked(kslot, 1 - half) + unpacked(gslot.at[0], 0) + unpacked(gslot.at[1], 1)
    nt[half, yat, 0, zhi] = summed.astype(BF16)
    z_copies = []
    for o in (2, 1, 3):
        at = nt.at[half, yat, 0, zhi]
        copy = remote(at, at, z_send.at[o], z_recv.at[o], (row, 4 * ((zhi + o) % 4) + yat))
        copy.start()
        z_copies.append(copy)

    @pl.when(row == col)
    def _():
        dcol[...] = dvec[...]
        for copy in d_copies:
            copy.start()


    for o in range(1, 4):
        at = nt.at[half, yat, 0, (zhi + 4 - o) % 4]
        remote(at, at, z_send.at[o], z_recv.at[o], (sibling, col)).wait_recv()
    xhigh, xlow, zlo = chip // 4, chip // 2 % 2, chip % 2

    def flipped(bit, by):
        return 1 - bit if by else bit

    def at_offset(m):
        return 4 * flipped(xhigh, m // 4) + 2 * flipped(xlow, m // 2 % 2) + flipped(zlo, m % 2)

    b_copies = []
    for m in range(1, 8):
        copy = remote(
            nt.at[half, yat, 0], nt.at[half, yat, m], b_send.at[m], b_recv.at[m], (2 * at_offset(m) + half, col)
        )
        copy.start()
        b_copies.append(copy)

    def piece(h, y, p):
        return nt.at[h, y, p] if p < 2 else nt.at[h, y, pl.ds(2, 6), p - 2]

    y_copies = []
    m_copies = []

    def send_piece(p):
        at = piece(half, yat, p)
        copies = [
            remote(at, at, y_send.at[p, o], y_recv.at[p, o], (row, 4 * zhi + (yat + o) % 4)) for o in (2, 1, 3)
        ]
        copies.append(remote(at, at, s_send.at[p, 0], s_recv.at[p, 0], (sibling, col)))
        for copy in copies:
            copy.start()
        y_copies.append(copies)

    def take_pieces(pieces):
        for p in pieces:
            for o in range(1, 4):
                at = piece(half, (yat + 4 - o) % 4, p)
                remote(at, at, y_send.at[p, o], y_recv.at[p, o], (sibling, col)).wait_recv()
                copy = remote(at, at, s_send.at[p, o], s_recv.at[p, o], (sibling, col))
                copy.start()
                m_copies.append(copy)
        for p in pieces:
            for o in range(4):
                at = piece(1 - half, (yat + 4 - o) % 4, p)
                remote(at, at, s_send.at[p, o], s_recv.at[p, o], (sibling, col)).wait_recv()

    def factors_here(part):
        f_copies[part][15].wait()
        for copy in f_copies[part][:15]:
            copy.wait_recv()

    send_piece(0)
    b_copies[0].wait_recv()
    send_piece(1)
    send_factors(1)
    for copy in b_copies[1:]:
        copy.wait_recv()
    send_piece(2)
    send_piece(3)
    send_factors(2)

    @pl.when(row != col)
    def _():
        d_copies[0].wait_recv()

    scale = jnp.concatenate([dcol[...], dcol[...]], axis=1)
    diagonal = jnp.zeros((256, 256), F32)
    for g in range(3):
        plain = jnp.concatenate([sbuf[r, g] for r in range(16)], axis=0)
        scaled = jnp.concatenate([sbuf[r, g] * scale for r in range(16)], axis=0)
        diagonal = diagonal + product(scaled, plain, TN)
    acc[:, 256:512] = diagonal

    plan = (
        ((0, 0),),
        ((1, 0), (0, 1), (1, 1)),
        ((2, 0), (2, 1)),
        ((3, 0), (3, 1), (0, 2), (1, 2), (2, 2), (3, 2)),
    )
    arrived = set()
    for i in range(4):
        if i < 2:
            for copy in y_copies[2 + i]:
                copy.wait_send()
            send_piece(4 + i)
        take_pieces((0, 1, 2) if i == 0 else (2 + i,))
        split_rows(i, chip, irrep, of_lane, nt, u0, u3, u1)
        for k, g in plan[i]:
            if g not in arrived:
                arrived.add(g)
                factors_here(g)
            row_sums(k, fm.at[g], u0, u3, u1, acc)
    for p in (0, 1, 4, 5):
        m_copies += y_copies[p]

    sums = []
    for p in range(3):
        total = jnp.zeros((64, 64), F32)
        for k in range(4):
            total = total + acc[64 * k : 64 * k + 64, 256 * p + 64 * k : 256 * p + 64 * k + 64]
        sums.append(total)
    near = (sums[0] + sums[0].T, sums[2].T, sums[2], sums[1] + sums[1].T)
    for r in range(16):
        for p in range(4):
            send_a[r, 4 * p : 4 * p + 4, :] = near[p][4 * r : 4 * r + 4, :]
    a_copies = []
    for o in range(1, 16):
        dest = (row + o) % 16
        copy = remote(send_a.at[dest], recv_a.at[o], sa.at[o], ra.at[o], (dest, col))
        copy.start()
        a_copies.append(copy)
    total = send_a[row]
    for o in range(1, 16):
        a_copies[o - 1].wait_recv()
        total = total + recv_a[o]
    turned = total.T
    for c in range(16):
        send_b[c] = turned[4 * c : 4 * c + 4, :]
    c_copies = []
    for o in range(1, 16):
        dest = (col + o) % 16
        copy = remote(send_b.at[dest], recv_b.at[o], sb.at[o], rb.at[o], (row, dest))
        copy.start()
        c_copies.append(copy)
    final = send_b[col]
    for o in range(1, 16):
        c_copies[o - 1].wait_recv()
        final = final + recv_b[o]
    back = final.T
    for p in range(4):
        out[p] = back[4 * p : 4 * p + 4, :]

    k_copy.wait_send()

    @pl.when(row != col)
    def _():
        for copy in g_copies:
            copy.wait_send()

    @pl.when(row == col)
    def _():
        for copy in d_copies:
            copy.wait_send()

    for copies in (f_copies[0][:15], f_copies[1][:15], f_copies[2][:15], b_copies, z_copies, m_copies,
                   a_copies, c_copies):
        for copy in copies:
            copy.wait_send()


def per_device(amplitudes, factors, tile_mask, tile_irrep):
    place = pl.BlockSpec(memory_space=pltpu.HBM)
    dma = pltpu.SemaphoreType.DMA
    return pl.pallas_call(
        kernel,
        out_shape=jax.ShapeDtypeStruct((4, 4, 4), F32),
        in_specs=[place] * 4,
        out_specs=pl.BlockSpec(memory_space=pltpu.VMEM),
        scratch_shapes=[
            pltpu.SMEM((16, 16), jnp.int32),
            pltpu.SMEM((16,), jnp.int32),
            pltpu.VMEM((4, 64, 64), BF16),
            pltpu.VMEM((192, 4096), BF16),
            pltpu.VMEM((16, 3, 64, 256), BF16),
            pltpu.VMEM((3, 1024, 256), BF16),
            pltpu.VMEM((2, 32, 128), F32),
            pltpu.VMEM((2, 16, 128), BF16),
            pltpu.VMEM((2, 16, 128), BF16),
            pltpu.VMEM((16, 128), BF16),
            pltpu.VMEM((2, 16, 128), BF16),
            pltpu.VMEM((64, 128), BF16),
            pltpu.VMEM((64, 128), BF16),
            pltpu.VMEM((2, 4, 8, 4, 32, 128), BF16),
            pltpu.VMEM((1024, 1024), BF16),
            pltpu.VMEM((1024, 1024), BF16),
            pltpu.VMEM((1024, 1024), BF16),
            pltpu.VMEM((256, 768), F32),
            pltpu.VMEM((16, 16, 64), F32),
            pltpu.VMEM((16, 16, 64), F32),
            pltpu.VMEM((16, 4, 16), F32),
            pltpu.VMEM((16, 4, 16), F32),
            dma((6,)), dma((3, 16)), dma((3, 16)), dma((3,)), dma((2,)), dma((2,)), dma((2,)),
            dma((16,)), dma(()), dma((8,)), dma((8,)),
            dma((4,)), dma((4,)), dma((6, 4)), dma((6, 4)), dma((6, 4)), dma((6, 4)),
            dma((16,)), dma((16,)), dma((16,)), dma((16,)),
        ],
        compiler_params=pltpu.CompilerParams(collective_id=0, has_side_effects=True, vmem_limit_bytes=62 << 20),
        name="ladder",
    )(tile_mask, tile_irrep, amplitudes, factors)


def solution(mesh):
    return jax.shard_map(
        per_device,
        mesh=mesh,
        in_specs=(P(None, "row", "col"), P("col", "row"), P(), P()),
        out_specs=P(None, "row", "col"),
        check_vma=False,
    )
```
